32 devices in a mesh: dp: 4 (over z), row: 4 (over y, x), col: 2 (over core).
Axes of the slice: x: 2, y: 2, z: 4, core: 2. Of those that a mesh axis runs over, the one named last changes fastest.
Arguments:
- block_input: bfloat16 [4096, 1024], P(('dp', 'row'), 'col'), may hold values from -20 to 20
- output_grad: bfloat16 [4096, 1024], P(('dp', 'row'), 'col'), may hold values from -6 to 6
- document_ids: int32 [4, 1024], P('dp'), may hold values from 0 to 3, never falling along the last dimension, each value on 1 to 512 neighbouring positions
- mixer_gain: bfloat16 [1024], P('col'), may hold values from 0.25 to 1.75
- mamba_gate: bfloat16 [1024, 1536], P('col', 'row'), may hold values from -0.1875 to 0.1875
- mamba_input: bfloat16 [1024, 1536], P('col', 'row'), may hold values from -0.1875 to 0.1875
- mamba_step: bfloat16 [1024, 24], P('col', 'row'), may hold values from -0.1875 to 0.1875
- query_weight: bfloat16 [1024, 512], P('col', 'row'), may hold values from -0.1875 to 0.1875
- key_weight: bfloat16 [1024, 128], P('col'), may hold values from -0.1875 to 0.1875
- value_weight: bfloat16 [1024, 128], P('col'), may hold values from -0.1875 to 0.1875
- state_weight: bfloat16 [1024, 256], P('col'), may hold values from -0.1875 to 0.1875
- input_filter: bfloat16 [1536, 4], P(('row', 'col')), may hold values from -3 to 3
- input_shift: bfloat16 [1536], P(('row', 'col')), may hold values from -0.5 to 0.5
- state_filter: bfloat16 [256, 4], replicated, may hold values from -3 to 3
- state_shift: bfloat16 [256], replicated, may hold values from -0.5 to 0.5
- step_bias: bfloat16 [24], P(('row', 'col')), may hold values from -5 to -1
- decay_log: bfloat16 [24], P(('row', 'col')), may hold values from 0 to 2.6875
- skip_gain: bfloat16 [24], P(('row', 'col')), may hold values from 0.5 to 1.5
- mixer_out: bfloat16 [2048, 1024], P('row', 'col'), may hold values from -4 to 4
- feed_gain: bfloat16 [1024], P('col'), may hold values from 0.25 to 1.75
- feed_gate: bfloat16 [1024, 2048], P('col', 'row'), may hold values from -0.1875 to 0.1875
- feed_up: bfloat16 [1024, 2048], P('col', 'row'), may hold values from -0.1875 to 0.1875
- feed_down: bfloat16 [2048, 1024], P('row', 'col'), may hold values from -0.125 to 0.125
Outputs:
- block_output: float32 [4096, 1024], P(('dp', 'row'), 'col')
- input_grad: float32 [4096, 1024], P(('dp', 'row'), 'col')
- mixer_gain_gradient: float32 [1024], P('col')
- mamba_gate_gradient: float32 [1024, 1536], P('col', 'row')
- mamba_input_gradient: float32 [1024, 1536], P('col', 'row')
- mamba_step_gradient: float32 [1024, 24], P('col', 'row')
- query_weight_gradient: float32 [1024, 512], P('col', 'row')
- key_weight_gradient: float32 [1024, 128], P('col')
- value_weight_gradient: float32 [1024, 128], P('col')
- state_weight_gradient: float32 [1024, 256], P('col')
- input_filter_gradient: float32 [1536, 4], P(('row', 'col'))
- input_shift_gradient: float32 [1536], P(('row', 'col'))
- state_filter_gradient: float32 [256, 4], replicated
- state_shift_gradient: float32 [256], replicated
- step_bias_gradient: float32 [24], P(('row', 'col'))
- decay_log_gradient: float32 [24], P(('row', 'col'))
- skip_gain_gradient: float32 [24], P(('row', 'col'))
- mixer_out_gradient: float32 [2048, 1024], P('row', 'col')
- feed_gain_gradient: float32 [1024], P('col')
- feed_gate_gradient: float32 [1024, 2048], P('col', 'row')
- feed_up_gradient: float32 [1024, 2048], P('col', 'row')
- feed_down_gradient: float32 [2048, 1024], P('row', 'col')
The draws below stay inside these ranges and needn't reach their ends.
Inputs may be any that keep to these rules, and one draw needn't show every extreme that they name: `document_ids`: along a sequence the document number never falls; each document is a run of one to half of 1024 tokens, and one run in each sequence is exactly that long.
All inputs are finite; a program needn't handle non-finite values.
Results may differ from the reference program's by a relative error of at most 0.039.
Values may be sent and summed in bfloat16 or wider, within the bound.
No kernel may reach another device: no remote copies, remote signals or barrier semaphores. Data moves between devices by JAX's collectives and lax.ppermute only.
A program may use at most 128 MiB of HBM per device.

```python
import math
import jax
import jax.numpy as jnp
import numpy as np
from jax import lax

D = 1024
HM = 24
HD = 64
N = 128
QH = 8
KVH = 2
FF = 2048
KCONV = 4
L = 1024
STRETCH = 256
DOCS = 4
DSSM = 1536
HPD = 3
SEQUENCES = 4
TOKENS = 4096
N_COL = 2


def draw_block_input(key, part):
    keys = jax.random.split(key, 3)
    column = jnp.arange(D).astype(jnp.float32) / D
    column_scale = 0.5 * 3.0 ** column * jax.random.uniform(keys[0], (D,), minval=0.8, maxval=1.25)
    row_scale = jnp.exp(jax.random.uniform(keys[1], (TOKENS, 1), minval=-1.2, maxval=0.5))
    base = jnp.clip(jax.random.normal(keys[2], (TOKENS, D)), -5.0, 5.0)
    return (base * column_scale * row_scale).astype(jnp.bfloat16)


def draw_mixer_out(key, part):
    span = HPD * HD + HD
    index = jnp.arange(DSSM + QH * HD) % span
    scale = jnp.where(index >= HPD * HD, (QH * HD / 64.0) ** (-0.5), DSSM ** (-0.5))
    values = jax.random.normal(key, (DSSM + QH * HD, D)) * scale[:, None]
    return values.astype(jnp.bfloat16)


def block_scale(key, shape, cuts, least, high):
    def one(dim, blocks):
        steps = jax.random.uniform(jax.random.fold_in(jax.random.fold_in(key, 6), dim), (blocks,), jnp.float32, least / len(cuts), high / len(cuts))
        return jnp.repeat(jnp.exp(steps), shape[dim] // blocks).reshape((-1,) + (1,) * (len(shape) - dim - 1))

    factor_of = one(*cuts[0])
    for cut in cuts[1:]:
        factor_of = factor_of * one(*cut)
    return factor_of


def split_up(number_of, total, most, lean):
    loads = [(1 << 20) // math.isqrt(standing ** lean) + 1 for standing in range(2, number_of + 1)]
    rest, counts = total - most - (number_of - 1), [1] * (number_of - 1)
    while rest > 0:
        free = [i for i in range(number_of - 1) if counts[i] < most]
        pool, remaining = sum([loads[i] for i in free]), rest
        for i in free:
            extra = min(most - counts[i], max(1, remaining * loads[i] // pool), rest)
            counts[i] = counts[i] + extra
            rest = rest - extra
    return np.array([most] + counts)


def ragged_sizes(stream_key, count, total, reach, slope):
    if count == 2:
        one = jax.random.randint(stream_key, (), max(1, total - reach), min(reach, total - 1) + 1)
        return jnp.stack([one, total - one])
    lengths = jnp.asarray(split_up(count, total, reach, slope), jnp.int32)
    twos = (count - 1) // 2
    source_of, receiver = lengths[1:1 + 2 * twos:2], lengths[2:2 + 2 * twos:2]
    room = jnp.minimum(source_of - 1, reach - receiver)
    shifted = jax.random.randint(jax.random.fold_in(stream_key, 1), (twos,), 0, 1 << 20) % (room + 1)
    lengths = lengths.at[1:1 + 2 * twos:2].set(source_of - shifted).at[2:2 + 2 * twos:2].set(receiver + shifted)
    return lengths[jax.random.permutation(jax.random.fold_in(stream_key, 2), count)]


def noise(own_key, dims, scale, bound, cuts=(), kind=jnp.bfloat16):
    drawn = scale * jax.random.normal(own_key, dims, jnp.float32)
    if cuts:
        drawn = drawn * block_scale(own_key, dims, cuts, -0.22, 0.18)
    return jnp.clip(drawn, -bound, bound).astype(kind)


def setup_inputs(seed: int = 0) -> dict:
    streams_of = jax.random.split(jax.random.key(seed), 24)
    block_input = draw_block_input(jax.random.fold_in(streams_of[23], 71), 0)
    output_grad = noise(streams_of[1], (TOKENS, D), 1.0, 6.0, ((0, 16), (1, 2)))
    document_ids = jax.vmap(lambda own: jnp.searchsorted(jnp.cumsum(ragged_sizes(own, DOCS, L, L // 2, 2)), jnp.arange(L), side="right"))(jax.random.split(streams_of[2], SEQUENCES)).reshape((SEQUENCES, L)).astype(jnp.int32)
    mixer_gain = jnp.clip(1.0 + 0.15 * jax.random.normal(streams_of[3], (D,), jnp.float32), 0.25, 1.75).astype(jnp.bfloat16)
    mamba_gate = noise(streams_of[4], (D, DSSM), D ** -0.5, 0.1875, ((0, 2), (1, 4)))
    mamba_input = noise(streams_of[5], (D, DSSM), D ** -0.5, 0.1875, ((0, 2), (1, 4)))
    mamba_step = noise(streams_of[6], (D, HM), D ** -0.5, 0.1875, ((0, 2), (1, 4)))
    query_weight = noise(streams_of[7], (D, QH * HD), D ** -0.5, 0.1875, ((0, 2), (1, 4)))
    key_weight = noise(streams_of[8], (D, KVH * HD), D ** -0.5, 0.1875, ((0, 2),))
    value_weight = noise(streams_of[9], (D, KVH * HD), D ** -0.5, 0.1875, ((0, 2),))
    state_weight = noise(streams_of[10], (D, 2 * N), D ** -0.5, 0.1875, ((0, 2),))
    input_filter = noise(streams_of[11], (DSSM, KCONV), KCONV ** -0.5, 3.0, ((0, 8),))
    input_shift = jnp.clip(jax.random.uniform(streams_of[12], (DSSM,), jnp.float32, -0.5, 0.5) * block_scale(streams_of[12], (DSSM,), ((0, 8),), -0.4, 0.0), -0.5, 0.5).astype(jnp.bfloat16)
    state_filter = noise(streams_of[13], (2 * N, KCONV), KCONV ** -0.5, 3.0)
    state_shift = jnp.clip(jax.random.uniform(streams_of[14], (2 * N,), jnp.float32, -0.5, 0.5), -0.5, 0.5).astype(jnp.bfloat16)
    step_bias = jnp.clip(-5.0 + 4.0 * jax.random.uniform(streams_of[15], (HM,), jnp.float32) ** block_scale(streams_of[15], (HM,), ((0, 8),), -0.2, 0.2), -5.0, -1.0).astype(jnp.bfloat16)
    decay_log = jnp.clip(2.6875 * jax.random.uniform(streams_of[16], (HM,), jnp.float32) ** block_scale(streams_of[16], (HM,), ((0, 8),), -0.2, 0.2), 0.0, 2.6875).astype(jnp.bfloat16)
    skip_gain = jnp.clip(0.5 + 1.0 * jax.random.uniform(streams_of[17], (HM,), jnp.float32) ** block_scale(streams_of[17], (HM,), ((0, 8),), -0.2, 0.2), 0.5, 1.5).astype(jnp.bfloat16)
    mixer_out = draw_mixer_out(jax.random.fold_in(streams_of[23], 71), 0)
    feed_gain = jnp.clip(1.0 + 0.15 * jax.random.normal(streams_of[19], (D,), jnp.float32), 0.25, 1.75).astype(jnp.bfloat16)
    feed_gate = noise(streams_of[20], (D, FF), D ** -0.5, 0.1875, ((0, 2), (1, 4)))
    feed_up = noise(streams_of[21], (D, FF), D ** -0.5, 0.1875, ((0, 2), (1, 4)))
    feed_down = noise(streams_of[22], (FF, D), FF ** -0.5, 0.125, ((0, 4), (1, 2)))
    return dict(block_input=block_input, output_grad=output_grad, document_ids=document_ids, mixer_gain=mixer_gain, mamba_gate=mamba_gate, mamba_input=mamba_input, mamba_step=mamba_step, query_weight=query_weight, key_weight=key_weight, value_weight=value_weight, state_weight=state_weight, input_filter=input_filter, input_shift=input_shift, state_filter=state_filter, state_shift=state_shift, step_bias=step_bias, decay_log=decay_log, skip_gain=skip_gain, mixer_out=mixer_out, feed_gain=feed_gain, feed_gate=feed_gate, feed_up=feed_up, feed_down=feed_down)


@jax.custom_vjp
def low(v):
    return lax.optimization_barrier(v.astype(jnp.bfloat16)).astype(jnp.float32)

@jax.custom_vjp
def low_back(v):
    return v

def low_keep(v):
    return (low(v), None)

def low_pass(kept, grad):
    return (grad,)

def back_keep(v):
    return (v, None)

def back_low(kept, grad):
    return (low(grad),)
low.defvjp(low_keep, low_pass)
low_back.defvjp(back_keep, back_low)
EPS = 1e-05
ROPE_BASE = 100000000000.0
HIGH = lax.Precision.HIGHEST

def matmul(left, right):
    return jnp.dot(left, right, precision=HIGH)

def normalize(values, gain):
    return values * lax.rsqrt(lax.optimization_barrier(jnp.mean(values * values, axis=-1, keepdims=True)) + EPS) * gain

def causal_filter(values, weight, shift):
    taps = weight.shape[1]
    length = values.shape[1]
    padded = jnp.pad(values, ((0, 0), (taps - 1, 0), (0, 0)))
    result = shift + padded[:, 0:length] * weight[:, 0]
    for index in range(1, taps):
        result = result + padded[:, index:index + length] * weight[:, index]
    return result

def rotate(values, sign):
    length = values.shape[-3]
    width = values.shape[-1]
    half = width // 2
    place = jnp.arange(length).astype(values.dtype)
    rates = ROPE_BASE ** (-2.0 * jnp.arange(half).astype(values.dtype) / width)
    angle = place[:, None] * rates[None, :]
    cosine = jnp.cos(angle)[:, None, :]
    sine = sign * jnp.sin(angle)[:, None, :]
    first = values[..., :half]
    second = values[..., half:]
    return jnp.concatenate([first * cosine - second * sine, second * cosine + first * sine], axis=-1)

def ssd_scan(inputs, steps, rates, inject, readout, segment):
    length, heads, width = inputs.shape
    states = inject.shape[1]
    blocks = length // STRETCH
    place = jnp.arange(STRETCH)
    before = place[:, None] >= place[None, :]

    def advance(carry, piece):
        state, last_doc = carry
        part_in, part_step, part_inject, part_read, part_doc = piece
        logs = jnp.cumsum(part_step * rates, axis=0)
        allowed = ((part_doc[:, None] == part_doc[None, :]) & before)[:, :, None]
        spread = jnp.where(allowed, logs[:, None, :] - logs[None, :, :], 0.0)
        decay = jnp.where(allowed, jnp.exp(spread), 0.0)
        intersection = jnp.dot(part_read, part_inject.T, precision=HIGH)
        mixing = intersection[:, :, None] * decay * part_step[None, :, :]
        inner = jnp.einsum('tsh,shp->thp', mixing, part_in, precision=HIGH)
        keep = (part_doc == last_doc).astype(part_in.dtype)
        carried = jnp.einsum('tn,hnp->thp', part_read, state, precision=HIGH) * (jnp.exp(logs) * keep[:, None])[:, :, None]
        end_doc = part_doc[STRETCH - 1]
        tail = (part_doc == end_doc).astype(part_in.dtype)
        towards = jnp.exp(logs[STRETCH - 1][None, :] - logs) * tail[:, None] * part_step
        going = jnp.exp(logs[STRETCH - 1]) * (end_doc == last_doc).astype(part_in.dtype)
        state = state * going[:, None, None] + jnp.einsum('sh,sn,shp->hnp', towards, part_inject, part_in, precision=HIGH)
        return ((state, end_doc), inner + carried)

    def split(values):
        return values.reshape((blocks, STRETCH) + values.shape[1:])
    start = (jnp.zeros((heads, states, width), inputs.dtype), jnp.int32(-1))
    final, outputs = lax.scan(jax.checkpoint(advance), start, (split(inputs), split(steps), split(inject), split(readout), split(segment)))
    return outputs.reshape(length, heads, width)

def mamba_piece(segment, input_values, gate_values, step_values, state_conv, filter_weight, filter_shift, step_bias, decay_log, skip_gain):
    sequences, length = segment.shape
    heads = step_values.shape[1]
    channels = input_values.shape[1]
    width = channels // heads
    states = state_conv.shape[1] // 2
    filtered = jax.nn.silu(causal_filter(input_values.reshape(sequences, length, channels), filter_weight, filter_shift))
    filtered = filtered.reshape(sequences, length, heads, width)
    steps = jax.nn.softplus(step_values + step_bias).reshape(sequences, length, heads)
    rates = -jnp.exp(decay_log)
    shared = state_conv.reshape(sequences, length, 2 * states)
    mixed = jax.vmap(ssd_scan, in_axes=(0, 0, None, 0, 0, 0))(filtered, steps, rates, shared[..., :states], shared[..., states:], segment)
    mixed = mixed + skip_gain[:, None] * filtered
    return mixed.reshape(sequences * length, channels) * jax.nn.silu(gate_values)

def block_partials(normed, weight):
    length = normed.shape[0]
    width = normed.shape[1] // N_COL
    parts = jnp.einsum('lcd,cdf->clf', normed.reshape(length, N_COL, width), weight.reshape(N_COL, width, weight.shape[1]), precision=HIGH)
    return lax.optimization_barrier(jnp.sum(low(parts), axis=0))

def attention(query, keys, values, segment):
    group = QH // KVH
    keys_all = jnp.repeat(keys, group, axis=1)
    values_all = jnp.repeat(values, group, axis=1)
    raw = low_back(jnp.einsum('qhd,khd->hqk', query, keys_all, precision=HIGH))
    place = jnp.arange(query.shape[0])
    allowed = (segment[:, None] == segment[None, :]) & (place[:, None] >= place[None, :])
    scores = jnp.where(allowed[None], raw * HD ** (-0.5), -1e+30)
    probs = low(jax.nn.softmax(scores, axis=-1))
    return jnp.einsum('hqk,khd->qhd', probs, values_all, precision=HIGH)

def layer(params, inputs, segment):
    mixer_gain, mamba_gate, mamba_input, mamba_step, query_weight, key_weight, value_weight, state_weight, input_filter, input_shift, state_filter, state_shift, step_bias, decay_log, skip_gain, mixer_out, feed_gain, feed_gate, feed_up, feed_down = params
    length = inputs.shape[0]
    normed = low(normalize(inputs, mixer_gain))
    gate_values = low_back(matmul(normed, mamba_gate))
    input_values = low_back(matmul(normed, mamba_input))
    step_values = low_back(matmul(normed, mamba_step))
    query_pre = low_back(matmul(normed, query_weight))
    state_raw = block_partials(normed, state_weight)
    key_raw = block_partials(normed, key_weight)
    value_raw = block_partials(normed, value_weight)
    state_conv = jax.nn.silu(causal_filter(state_raw[None], state_filter, state_shift))[0]
    gated = mamba_piece(segment[None], input_values, gate_values, step_values, state_conv, input_filter, input_shift, step_bias, decay_log, skip_gain)
    query = low(rotate(query_pre.reshape(length, QH, HD), 1.0))
    keys = low(rotate(key_raw.reshape(length, KVH, HD), 1.0))
    values = low(value_raw.reshape(length, KVH, HD))
    attended = attention(query, keys, values, segment)
    gated_low = low_back(low(gated))
    attended_low = low_back(low(attended.reshape(length, QH * HD)))
    features = jnp.concatenate([gated_low.reshape(length, QH, HPD * HD), attended_low.reshape(length, QH, HD)], axis=2)
    features = features.reshape(length, DSSM + QH * HD)
    after_mixer = inputs + low_back(matmul(features, mixer_out))
    normed_two = low(normalize(after_mixer, feed_gain))
    gate = low_back(matmul(normed_two, feed_gate))
    upper = low_back(matmul(normed_two, feed_up))
    hidden = low_back(low(jax.nn.silu(gate) * upper))
    return after_mixer + low_back(matmul(hidden, feed_down))

def reference(block_input, output_grad, document_ids, mixer_gain, mamba_gate, mamba_input, mamba_step, query_weight, key_weight, value_weight, state_weight, input_filter, input_shift, state_filter, state_shift, step_bias, decay_log, skip_gain, mixer_out, feed_gain, feed_gate, feed_up, feed_down):
    params = tuple((item.astype(jnp.float32) for item in (mixer_gain, mamba_gate, mamba_input, mamba_step, query_weight, key_weight, value_weight, state_weight, input_filter, input_shift, state_filter, state_shift, step_bias, decay_log, skip_gain, mixer_out, feed_gain, feed_gate, feed_up, feed_down)))
    inputs = block_input.astype(jnp.float32).reshape(-1, L, D)
    cotangent = output_grad.astype(jnp.float32).reshape(-1, L, D)

    def one(carry, item):
        sequence, upstream, segment = item

        def apply(weights, values):
            return layer(weights, values, segment)
        output, pull = jax.vjp(apply, params, sequence)
        weight_grads, input_part = pull(upstream)
        return (jax.tree.map(jnp.add, carry, weight_grads), (output, input_part))
    zeros = jax.tree.map(jnp.zeros_like, params)
    total, (outputs, input_parts) = lax.scan(one, zeros, (inputs, cotangent, document_ids))
    return (outputs.reshape(-1, D), input_parts.reshape(-1, D), total[0], total[1], total[2], total[3], total[4], total[5], total[6], total[7], total[8], total[9], total[10], total[11], total[12], total[13], total[14], total[15], total[16], total[17], total[18], total[19])
```

```python
import numpy as np
import jax
import jax.numpy as jnp
from jax import lax
from jax.experimental import pallas as pl
from jax.experimental.pallas import tpu as pltpu
from jax.sharding import PartitionSpec as P
from functools import partial

D = 1024
HD = 64
QH = 8
KVH = 2
STRETCH = 256
EPS = 1e-05
ROPE_BASE = 100000000000.0
HIGH = lax.Precision.HIGHEST


def product(left, right):
    return jnp.dot(left, right, preferred_element_type=jnp.float32)


def against(left, right):
    return lax.dot_general(
        left, right, (((1,), (1,)), ((), ())), preferred_element_type=jnp.float32
    )


def outer(left, right):
    return lax.dot_general(
        left, right, (((0,), (0,)), ((), ())), preferred_element_type=jnp.float32
    )


def tri_masks(size):
    row = lax.broadcasted_iota(jnp.int32, (size, size), 0)
    col = lax.broadcasted_iota(jnp.int32, (size, size), 1)
    return row, col


def precise(left, right):
    return jnp.dot(left, right, precision=HIGH, preferred_element_type=jnp.float32)


def low(values):
    return values.astype(jnp.bfloat16)


def silu_slope(values, sigma):
    return sigma * (1.0 + values * (1.0 - sigma))


def by_head(values, lanes, heads, width):
    result = values[:, heads - 1 : heads]
    for head in range(heads - 2, -1, -1):
        result = jnp.where(lanes < (head + 1) * width, values[:, head : head + 1], result)
    return result


def filtered(padded, weights, first, count, taps):
    result = weights[taps : taps + 1, :] + padded[pl.ds(first + 9 - taps, count), :] * weights[0:1, :]
    for tap in range(1, taps):
        result = result + padded[pl.ds(first + 9 - taps + tap, count), :] * weights[tap : tap + 1, :]
    return result


def block_terms(block, size, refs, heads):
    step_col, log_col, step_row, log_row, doc_col, doc_row = refs
    rows = slice(block * size, (block + 1) * size)
    at, of = tri_masks(size)
    lower = (at >= of).astype(jnp.float32)
    upper = (at <= of).astype(jnp.float32)
    logs_col = precise(lower, log_col[rows, :])
    logs_row = precise(log_row[:, rows], upper)
    docs = doc_col[rows, :]
    allowed = (docs == doc_row[:, rows]) & (at >= of)
    end_doc = doc_col[(block + 1) * size - 1 : (block + 1) * size, :]
    last_logs = logs_col[size - 1 : size, :]
    tail = (docs == end_doc).astype(jnp.float32)
    reach = jnp.exp(last_logs - logs_col) * tail
    if block == 0:
        carry_in = jnp.zeros_like(logs_col)
        going = jnp.zeros_like(last_logs)
    else:
        prior = doc_col[block * size - 1 : block * size, :]
        carry_in = jnp.exp(logs_col) * (docs == prior).astype(jnp.float32)
        going = jnp.exp(last_logs) * (end_doc == prior).astype(jnp.float32)
    decays = []
    for head in range(heads):
        spread = logs_col[:, head : head + 1] - logs_row[head : head + 1, :]
        decays.append(jnp.where(allowed, jnp.exp(jnp.where(allowed, spread, 0.0)), 0.0))
    return rows, decays, carry_in, reach, going, lower, upper


def fill_pads(pad_x, pad_s, x_ref, s_ref, length):
    pad_x[0:8, :] = jnp.zeros((8, pad_x.shape[1]), jnp.float32)
    pad_s[0:8, :] = jnp.zeros((8, pad_s.shape[1]), jnp.float32)
    pad_x[pl.ds(8, length), :] = x_ref[...].astype(jnp.float32)
    pad_s[pl.ds(8, length), :] = s_ref[...]


def mamba_forward_kernel(
    heads, taps, x_ref, z_ref, s_ref, step_col, log_col, step_row, log_row, doc_col, doc_row,
    wx_ref, ws_ref, skip_ref, gated_ref, mixed_ref, states_ref, pad_x, pad_s,
):
    length, channels = x_ref.shape
    width = channels // heads
    states = s_ref.shape[1] // 2
    size = min(STRETCH, length)
    fill_pads(pad_x, pad_s, x_ref, s_ref, length)
    lanes = lax.broadcasted_iota(jnp.int32, (1, channels), 1)
    wx, ws = wx_ref[...], ws_ref[...]
    state = jnp.zeros((states, channels), jnp.float32)
    refs = (step_col, log_col, step_row, log_row, doc_col, doc_row)
    for block in range(length // size):
        rows, decays, carry_in, reach, going, _, _ = block_terms(block, size, refs, heads)
        pre_x = filtered(pad_x, wx, block * size, size, taps)
        inner = pre_x * jax.nn.sigmoid(pre_x)
        pre_s = filtered(pad_s, ws, block * size, size, taps)
        conv = low(pre_s * jax.nn.sigmoid(pre_s))
        inject, readout = conv[:, :states], conv[:, states:]
        states_ref[block] = state
        overlap = against(readout, inject)
        mixed = product(readout, low(state)) * by_head(carry_in, lanes, heads, width)
        for head in range(heads):
            mixing = overlap * decays[head] * step_row[head : head + 1, rows]
            mine = (lanes >= head * width) & (lanes < (head + 1) * width)
            mixed = mixed + product(low(mixing), low(jnp.where(mine, inner, 0.0)))
        towards = by_head(reach * step_col[rows, :], lanes, heads, width)
        state = state * by_head(going, lanes, heads, width) + outer(inject, low(towards * inner))
        mixed = mixed + skip_ref[...] * inner
        mixed_ref[rows, :] = mixed
        gate = z_ref[rows, :].astype(jnp.float32)
        gated_ref[rows, :] = low(mixed * (gate * jax.nn.sigmoid(gate)))


def mamba_backward_kernel(
    heads, taps, x_ref, z_ref, s_ref, step_col, log_col, step_row, log_row, doc_col, doc_row,
    wx_ref, ws_ref, skip_ref, mixed_ref, states_ref, grad_ref,
    dx_ref, dz_ref, ds_ref, back_col, back_row, gx_ref, gs_ref,
    pad_x, pad_s, tail_x, tail_s,
):
    length, channels = x_ref.shape
    width = channels // heads
    double = s_ref.shape[1]
    states = double // 2
    size = min(STRETCH, length)
    fill_pads(pad_x, pad_s, x_ref, s_ref, length)
    tail_x[pl.ds(length, 8), :] = jnp.zeros((8, channels), jnp.float32)
    tail_s[pl.ds(length, 8), :] = jnp.zeros((8, double), jnp.float32)
    lanes = lax.broadcasted_iota(jnp.int32, (1, channels), 1)
    pick = (
        lax.broadcasted_iota(jnp.int32, (channels, 8), 0) // width
        == lax.broadcasted_iota(jnp.int32, (channels, 8), 1)
    ).astype(jnp.float32)
    lane8 = lax.broadcasted_iota(jnp.int32, (1, 8), 1)
    sub8 = lax.broadcasted_iota(jnp.int32, (8, 1), 0)
    wx, ws = wx_ref[...], ws_ref[...]
    skip = skip_ref[...]
    refs = (step_col, log_col, step_row, log_row, doc_col, doc_row)
    state_grad = jnp.zeros((states, channels), jnp.float32)
    skip_sum = jnp.zeros((1, channels), jnp.float32)
    for block in reversed(range(length // size)):
        rows, decays, carry_in, reach, going, lower, upper = block_terms(block, size, refs, heads)
        pre_x = filtered(pad_x, wx, block * size, size, taps)
        sigma_x = jax.nn.sigmoid(pre_x)
        inner = pre_x * sigma_x
        pre_s = filtered(pad_s, ws, block * size, size, taps)
        sigma_s = jax.nn.sigmoid(pre_s)
        conv = low(pre_s * sigma_s)
        inject, readout = conv[:, :states], conv[:, states:]
        gate = z_ref[rows, :].astype(jnp.float32)
        sigma_z = jax.nn.sigmoid(gate)
        grad = grad_ref[rows, :].astype(jnp.float32)
        dy = grad * (gate * sigma_z)
        dz_ref[rows, :] = low(grad * mixed_ref[rows, :] * silu_slope(gate, sigma_z))
        skip_sum = skip_sum + jnp.sum(dy * inner, axis=0, keepdims=True)
        before = states_ref[block]
        before_low, state_low = low(before), low(state_grad)
        overlap = against(readout, inject)
        inner_low = low(inner)
        carry_wide = by_head(carry_in, lanes, heads, width)
        reach_wide = by_head(reach, lanes, heads, width)
        step_wide = by_head(step_col[rows, :], lanes, heads, width)
        carried_grad = carry_wide * dy
        pushed = product(inject, state_low)
        dinner = skip * dy + reach_wide * step_wide * pushed
        overlap_grad = jnp.zeros((size, size), jnp.float32)
        logs_col = jnp.zeros((size, 8), jnp.float32)
        logs_row = jnp.zeros((8, size), jnp.float32)
        direct_row = jnp.zeros((8, size), jnp.float32)
        for head in range(heads):
            steps = step_row[head : head + 1, rows]
            mine = (lanes >= head * width) & (lanes < (head + 1) * width)
            dy_mine = low(jnp.where(mine, dy, 0.0))
            weighted = decays[head] * against(dy_mine, inner_low)
            overlap_grad = overlap_grad + weighted * steps
            linear = weighted * overlap
            summed = jnp.sum(linear, axis=0, keepdims=True)
            direct_row = jnp.where(sub8 == head, summed, direct_row)
            logs_row = jnp.where(sub8 == head, -(summed * steps), logs_row)
            across = jnp.sum(linear * steps, axis=1, keepdims=True)
            logs_col = jnp.where(lane8 == head, across, logs_col)
            mixing = overlap * decays[head] * steps
            dinner = dinner + outer(low(mixing), dy_mine)
        overlap_low = low(overlap_grad)
        dreadout = product(overlap_low, inject) + against(low(carried_grad), before_low)
        towards = reach_wide * step_wide * inner
        dinject = outer(overlap_low, readout) + against(low(towards), state_low)
        carried = precise(carried_grad * product(readout, before_low), pick)
        direct_col = precise(reach_wide * inner * pushed, pick)
        pulled = direct_col * step_col[rows, :]
        kept = precise(jnp.sum(before * state_grad, axis=0, keepdims=True), pick) * going
        logs_col = logs_col + carried - pulled
        ending = jnp.sum(pulled, axis=0, keepdims=True) + kept
        back_col[rows, 0:8] = precise(upper, logs_col) + ending
        back_col[rows, 8:16] = direct_col
        back_row[0:8, rows] = precise(logs_row, lower)
        back_row[8:16, rows] = direct_row
        state_grad = state_grad * by_head(going, lanes, heads, width) + outer(
            readout, low(carried_grad)
        )
        tail_x[rows, :] = dinner * silu_slope(pre_x, sigma_x)
        slope_s = silu_slope(pre_s, sigma_s)
        tail_s[rows, 0:states] = dinject * slope_s[:, :states]
        tail_s[rows, states:double] = dreadout * slope_s[:, states:]
    gx_ref[...] = jnp.zeros_like(gx_ref)
    gs_ref[...] = jnp.zeros_like(gs_ref)
    gx_ref[taps + 1 : taps + 2, :] = skip_sum
    for padded, tail, weights, out_ref, g_ref in (
        (pad_x, tail_x, wx, dx_ref, gx_ref),
        (pad_s, tail_s, ws, ds_ref, gs_ref),
    ):
        for block in range(length // size):
            first = block * size
            here = tail[pl.ds(first, size), :]
            total = here * weights[taps - 1 : taps, :]
            for tap in range(taps - 1):
                total = total + tail[pl.ds(first + taps - 1 - tap, size), :] * weights[tap : tap + 1, :]
            out_ref[pl.ds(first, size), :] = low(total)
            g_ref[taps : taps + 1, :] += jnp.sum(here, axis=0, keepdims=True)
            for tap in range(taps):
                moved = padded[pl.ds(first + 9 - taps + tap, size), :]
                g_ref[tap : tap + 1, :] += jnp.sum(here * moved, axis=0, keepdims=True)


def turn_matrix(width):
    row, col = tri_masks(width)
    half = width // 2
    return jnp.where(row == col + half, -1.0, jnp.where(col == row + half, 1.0, 0.0))


def score_block(block, size, query, keys, doc_col, doc_row, scale):
    count = (block + 1) * size
    at = block * size + lax.broadcasted_iota(jnp.int32, (size, count), 0)
    of = lax.broadcasted_iota(jnp.int32, (size, count), 1)
    allowed = (doc_col[block * size : count, :] == doc_row[:, 0:count]) & (at >= of)
    scores = jnp.where(allowed, against(query, keys[0:count, :]) * scale, -1e30)
    peak = jnp.max(scores, axis=1, keepdims=True)
    weights = jnp.exp(scores - peak)
    return weights / jnp.sum(weights, axis=1, keepdims=True)


def attend_forward_kernel(
    q_ref, k_ref, v_ref, cos_ref, sin_ref, doc_col, doc_row, out_ref, qr_ref, kr_ref
):
    length, width = q_ref.shape
    size = min(256, length)
    turn = turn_matrix(width)
    cosine, sine = cos_ref[...], sin_ref[...]
    query, keys = q_ref[...], k_ref[...]
    qr_ref[...] = low(query * cosine + precise(query, turn) * sine)
    kr_ref[...] = low(keys * cosine + precise(keys, turn) * sine)
    values = low(v_ref[...])
    for block in range(length // size):
        rows = slice(block * size, (block + 1) * size)
        probs = score_block(
            block, size, qr_ref[rows, :], kr_ref, doc_col, doc_row, width ** (-0.5)
        )
        out_ref[rows, :] = low(product(low(probs), values[0 : (block + 1) * size, :]))


def attend_backward_kernel(
    qr_ref, kr_ref, v_ref, cos_ref, sin_ref, doc_col, doc_row, grad_ref,
    dq_ref, dkv_ref, dk_acc, dv_acc,
):
    length, width = qr_ref.shape
    size = min(256, length)
    scale = width ** (-0.5)
    turn = turn_matrix(width)
    values = low(v_ref[...])
    dk_acc[...] = jnp.zeros_like(dk_acc)
    dv_acc[...] = jnp.zeros_like(dv_acc)
    for block in range(length // size):
        rows = slice(block * size, (block + 1) * size)
        count = (block + 1) * size
        query = qr_ref[rows, :]
        grad = grad_ref[rows, :]
        probs = score_block(block, size, query, kr_ref, doc_col, doc_row, scale)
        prob_grad = against(grad, values[0:count, :])
        inner = jnp.sum(probs * prob_grad, axis=1, keepdims=True)
        score_grad = low(probs * (prob_grad - inner) * scale)
        dq = product(score_grad, kr_ref[0:count, :])
        dq_ref[rows, :] = low(dq * cos_ref[rows, :] - precise(dq, turn) * sin_ref[rows, :])
        dk_acc[0:count, :] += outer(score_grad, query)
        dv_acc[0:count, :] += outer(low(probs), grad)
    dk = dk_acc[...]
    dkv_ref[:, 0:width] = low(dk * cos_ref[...] - precise(dk, turn) * sin_ref[...])
    dkv_ref[:, width : 2 * width] = low(dv_acc[...])


def whole_spec(array):
    shape = array.shape
    return pl.BlockSpec(shape, lambda step, rank=len(shape): (0,) * rank)


def part_spec(array):
    shape = array.shape
    return pl.BlockSpec((None,) + shape[1:], lambda step, rank=len(shape): (step,) + (0,) * (rank - 1))


def per_sequence(kernel, parts, wholes, tail_parts, outs, scratch, name):
    sequences = parts[0].shape[0]
    return pl.pallas_call(
        kernel,
        out_shape=outs,
        grid=(sequences,),
        in_specs=[part_spec(a) for a in parts]
        + [whole_spec(a) for a in wholes]
        + [part_spec(a) for a in tail_parts],
        out_specs=[part_spec(a) for a in outs],
        scratch_shapes=scratch,
        compiler_params=pltpu.CompilerParams(vmem_limit_bytes=50 * 1024 * 1024),
        name=name,
    )(*parts, *wholes, *tail_parts)


def swapped(values):
    return lax.ppermute(values, "col", [(0, 1), (1, 0)])


def across(values, axis, bit):
    count = lax.axis_size(axis)
    return lax.ppermute(values, axis, [(place, place ^ bit) for place in range(count)])


def in_order(own, other, axis):
    first = lax.axis_index("col") == 0
    return jnp.where(
        first, jnp.concatenate([own, other], axis), jnp.concatenate([other, own], axis)
    )


def row_gather(values):
    half = values.shape[0] // 2
    upper, lower = values[:half], values[half:]
    a = across(upper, "row", 1)
    b = across(lower, "row", 2)
    c = across(jnp.concatenate([upper, a]), "row", 2)
    d = across(jnp.concatenate([lower, b]), "row", 1)
    return jnp.concatenate([upper, lower, a, d[:half], c[:half], b, c[half:], d[half:]])


def row_reorder(values):
    count = lax.axis_size("row")
    size = values.shape[0] // count
    here = lax.axis_index("row")
    return jnp.concatenate(
        [lax.dynamic_slice_in_dim(values, (here ^ k) * size, size, 0) for k in range(count)]
    )


def row_scatter(values):
    size = values.shape[0] // 4
    half = values.shape[1] // 2
    part = values.reshape(4, size, values.shape[1])
    left, right = part[:, :, :half], part[:, :, half:]
    wide = jnp.float32
    r1 = across(jnp.stack([left[1], left[3]]), "row", 1).astype(wide)
    s1 = across(jnp.stack([right[2], right[3]]), "row", 2).astype(wide)
    r2 = across(low(left[2].astype(wide) + r1[1]), "row", 2).astype(wide)
    s2 = across(low(right[1].astype(wide) + s1[1]), "row", 1).astype(wide)
    return jnp.concatenate(
        [left[0].astype(wide) + r1[0] + r2, right[0].astype(wide) + s1[0] + s2], axis=1
    )


def dp_sum(values):
    count = lax.axis_size("dp")
    if count & (count - 1):
        return lax.psum(low(values), "dp").astype(jnp.float32)
    here = lax.axis_index("dp")
    bits = [1 << k for k in range(count.bit_length() - 1)]
    for bit in bits:
        half = values.shape[0] // 2
        side = (here // bit) % 2
        mine = lax.dynamic_slice_in_dim(values, side * half, half, 0)
        theirs = lax.dynamic_slice_in_dim(values, (1 - side) * half, half, 0)
        values = mine.astype(jnp.float32) + across(low(theirs), "dp", bit).astype(jnp.float32)
    values = low(values)
    for bit in reversed(bits):
        other = across(values, "dp", bit)
        first = (here // bit) % 2 == 0
        values = jnp.where(
            first, jnp.concatenate([values, other]), jnp.concatenate([other, values])
        )
    return values.astype(jnp.float32)


def vector_sum(values, axis):
    count = lax.axis_size(axis)
    if count > 4:
        return lax.psum(values, axis)
    here = lax.axis_index(axis)
    kept = jnp.zeros((count,) + values.shape, values.dtype)
    for bit in range(count):
        item = values if bit == 0 else across(values, axis, bit)
        kept = lax.dynamic_update_slice_in_dim(kept, item[None], here ^ bit, 0)
    total = kept[0]
    for place in range(1, count):
        total = total + kept[place]
    return total


def packed(parts):
    flat = jnp.concatenate([part.reshape(-1) for part in parts])
    return jnp.pad(flat, (0, -flat.shape[0] % 1024)).reshape(-1, 128)


def unpacked(values, shapes):
    flat = values.reshape(-1)
    result, first = [], 0
    for shape in shapes:
        count = int(np.prod(shape))
        result.append(flat[first : first + count].reshape(shape))
        first += count
    return result


def norm_forward(residual, gain):
    total = jnp.sum(residual * residual, axis=1)
    total = total + swapped(total)
    inverse = lax.rsqrt(total / D + EPS)
    return (low(residual * inverse[:, None] * gain), inverse)


def norm_backward(residual, inverse, gain, upstream):
    scaled = upstream * gain
    inner = jnp.sum(scaled * residual, axis=1)
    inner = inner + swapped(inner)
    input_part = inverse[:, None] * scaled - residual * (inverse**3 * inner / D)[:, None]
    gain_part = jnp.sum(upstream * residual * inverse[:, None], axis=0)
    return (input_part, gain_part)


def tables(weight, shift):
    taps = weight.shape[1]
    both = jnp.concatenate([weight.T, shift[None]], axis=0).astype(jnp.float32)
    return jnp.pad(both, ((0, 7 - taps), (0, 0)))


def cut(values, sequences):
    return values.reshape(sequences, values.shape[0] // sequences, values.shape[1])


def doc_views(document_ids):
    return (document_ids[:, :, None], document_ids[:, None, :])


def mamba_forward(
    document_ids, inputs, gates, step_values, state_raw, input_filter, input_shift,
    state_filter, state_shift, step_bias, decay_log, skip_gain,
):
    sequences, length = document_ids.shape
    heads = step_values.shape[1]
    channels = inputs.shape[1]
    double = state_raw.shape[1]
    taps = input_filter.shape[1]
    shifted = step_values + step_bias
    steps = jax.nn.softplus(shifted)
    rates = -jnp.exp(decay_log)
    step_col = cut(jnp.pad(steps, ((0, 0), (0, 8 - heads))), sequences)
    log_col = cut(jnp.pad(steps * rates, ((0, 0), (0, 8 - heads))), sequences)
    parts = [
        cut(inputs, sequences), cut(gates, sequences), cut(state_raw, sequences),
        step_col, log_col, step_col.swapaxes(1, 2), log_col.swapaxes(1, 2),
        *doc_views(document_ids),
    ]
    wholes = [
        tables(input_filter, input_shift),
        tables(state_filter, state_shift),
        jnp.repeat(skip_gain, channels // heads)[None],
    ]
    blocks = length // min(STRETCH, length)
    outs = (
        jax.ShapeDtypeStruct((sequences, length, channels), jnp.bfloat16),
        jax.ShapeDtypeStruct((sequences, length, channels), jnp.float32),
        jax.ShapeDtypeStruct((sequences, blocks, double // 2, channels), jnp.float32),
    )
    scratch = [
        pltpu.VMEM((length + 8, channels), jnp.float32),
        pltpu.VMEM((length + 8, double), jnp.float32),
    ]
    gated, mixed, states = per_sequence(
        partial(mamba_forward_kernel, heads, taps), parts, wholes, [], outs, scratch, "mamba_fwd"
    )
    saved = (parts, wholes, mixed, states, shifted, steps, rates)
    return gated.reshape(sequences * length, channels), saved


def mamba_backward(saved, grad, taps):
    parts, wholes, mixed, states, shifted, steps, rates = saved
    sequences, length, channels = mixed.shape
    heads = rates.shape[0]
    double = parts[2].shape[2]
    outs = (
        jax.ShapeDtypeStruct((sequences, length, channels), jnp.bfloat16),
        jax.ShapeDtypeStruct((sequences, length, channels), jnp.bfloat16),
        jax.ShapeDtypeStruct((sequences, length, double), jnp.bfloat16),
        jax.ShapeDtypeStruct((sequences, length, 16), jnp.float32),
        jax.ShapeDtypeStruct((sequences, 16, length), jnp.float32),
        jax.ShapeDtypeStruct((sequences, 8, channels), jnp.float32),
        jax.ShapeDtypeStruct((sequences, 8, double), jnp.float32),
    )
    scratch = [
        pltpu.VMEM((length + 8, channels), jnp.float32),
        pltpu.VMEM((length + 8, double), jnp.float32),
        pltpu.VMEM((length + 8, channels), jnp.float32),
        pltpu.VMEM((length + 8, double), jnp.float32),
    ]
    dx, dz, ds, back_col, back_row, gx, gs = per_sequence(
        partial(mamba_backward_kernel, heads, taps), parts, wholes,
        [mixed, states, cut(grad, sequences)], outs, scratch, "mamba_bwd",
    )
    tokens = sequences * length
    back = (back_col + back_row.swapaxes(1, 2)).reshape(tokens, 16)
    turned, direct = back[:, :heads], back[:, 8 : 8 + heads]
    step_back = (turned * rates + direct) * jax.nn.sigmoid(shifted)
    gx, gs = jnp.sum(gx, axis=0), jnp.sum(gs, axis=0)
    return (
        dx.reshape(tokens, channels),
        dz.reshape(tokens, channels),
        step_back,
        ds.reshape(tokens, double),
        gx[:taps].T,
        gx[taps],
        gs[:taps].T,
        gs[taps],
        jnp.sum(step_back, axis=0),
        rates * jnp.sum(steps * turned, axis=0),
        jnp.sum(gx[taps + 1].reshape(heads, channels // heads), axis=1),
    )


def rope_tables(length, width):
    rates = ROPE_BASE ** (-2.0 * np.arange(width // 2) / width)
    angle = np.arange(length)[:, None] * rates.astype(np.float32)[None, :]
    both = np.concatenate([angle, angle], axis=1)
    return [jnp.asarray(np.cos(both), jnp.float32), jnp.asarray(np.sin(both), jnp.float32)]


def attend_forward(document_ids, query, keys, values):
    sequences, length = document_ids.shape
    width = query.shape[1]
    shape = jax.ShapeDtypeStruct((sequences, length, width), jnp.bfloat16)
    attended, query_low, key_low = per_sequence(
        attend_forward_kernel,
        [cut(query, sequences), cut(keys, sequences), cut(values, sequences)],
        rope_tables(length, width),
        list(doc_views(document_ids)),
        (shape, shape, shape),
        [],
        "attend_fwd",
    )
    return attended.reshape(sequences * length, width), (query_low, key_low, cut(values, sequences))


def attend_backward(document_ids, saved, grad):
    sequences, length = document_ids.shape
    width = grad.shape[1]
    dq, dkv = per_sequence(
        attend_backward_kernel,
        list(saved),
        rope_tables(length, width),
        list(doc_views(document_ids)) + [cut(grad, sequences)],
        (
            jax.ShapeDtypeStruct((sequences, length, width), jnp.bfloat16),
            jax.ShapeDtypeStruct((sequences, length, 2 * width), jnp.bfloat16),
        ),
        [pltpu.VMEM((length, width), jnp.float32), pltpu.VMEM((length, width), jnp.float32)],
        "attend_bwd",
    )
    return dq.reshape(sequences * length, width), dkv.reshape(sequences * length, 2 * width)


def on_device(
    block_input, output_grad, document_ids, mixer_gain, mamba_gate, mamba_input, mamba_step,
    query_weight, key_weight, value_weight, state_weight, input_filter, input_shift,
    state_filter, state_shift, step_bias, decay_log, skip_gain, mixer_out, feed_gain,
    feed_gate, feed_up, feed_down,
):
    col = lax.axis_index("col")
    group_index = lax.axis_index("row") * 2 + col
    pair_head = group_index // (QH // KVH)
    heads = skip_gain.shape[0]
    channels = input_shift.shape[0]
    taps = input_filter.shape[1]
    double = state_weight.shape[1]
    wide = jnp.float32
    mixer_scale = mixer_gain.astype(wide)
    feed_scale = feed_gain.astype(wide)

    def half_of(weight, side, axis):
        size = weight.shape[axis] // 2
        return lax.dynamic_slice_in_dim(weight, side * size, size, axis)

    proj = (mamba_gate, mamba_input, query_weight, mamba_step)
    spans = [weight.shape[1] // 2 for weight in proj]
    spare = -sum(spans) % 128

    def proj_half(side):
        parts = [half_of(weight, side, 1) for weight in proj]
        return jnp.pad(jnp.concatenate(parts, axis=1), ((0, 0), (0, spare)))

    proj_own, proj_other = proj_half(col), proj_half(1 - col)
    common = jnp.concatenate(
        [
            state_weight,
            lax.dynamic_slice_in_dim(key_weight, pair_head * HD, HD, 1),
            lax.dynamic_slice_in_dim(value_weight, pair_head * HD, HD, 1),
        ],
        axis=1,
    )
    feed_both = jnp.concatenate(
        [jnp.concatenate([half_of(w, side, 1) for w in (feed_gate, feed_up)], axis=1)
         for side in (col, 1 - col)], axis=1,
    )
    feed_own, feed_other = jnp.split(feed_both, 2, axis=1)
    out_own, out_other = half_of(mixer_out, col, 0), half_of(mixer_out, 1 - col, 0)
    down_own, down_other = half_of(feed_down, col, 0), half_of(feed_down, 1 - col, 0)

    residual = block_input.astype(wide)
    normed_one, inverse_one = norm_forward(residual, mixer_scale)
    tokens_one = row_reorder(row_gather(normed_one))
    common_low = low(product(tokens_one, common))
    common_raw = common_low.astype(wide) + swapped(common_low).astype(wide)
    proj_sent = swapped(low(product(tokens_one, proj_other)))
    proj_raw = product(tokens_one, proj_own) + proj_sent.astype(wide)
    edges = np.cumsum([0] + spans)
    gate_values, input_values, query_pre, step_values = (
        proj_raw[:, edges[k] : edges[k + 1]] for k in range(4)
    )
    state_raw = common_raw[:, :double]
    key_raw, value_raw = common_raw[:, double : double + HD], common_raw[:, double + HD :]
    gated, mamba_saved = mamba_forward(
        document_ids, low(input_values), low(gate_values), step_values, state_raw,
        input_filter.astype(wide), input_shift.astype(wide), state_filter.astype(wide),
        state_shift.astype(wide), step_bias.astype(wide), decay_log.astype(wide),
        skip_gain.astype(wide),
    )
    attended, attend_saved = attend_forward(document_ids, query_pre, key_raw, value_raw)
    features = jnp.concatenate([gated, attended], axis=1)
    features_other = swapped(features)
    mixer_part = low(product(features, out_own) + product(features_other, out_other))
    after_mixer = residual + row_scatter(row_reorder(mixer_part))

    grad_tokens = row_gather(output_grad)
    hidden_sent = swapped(low(against(grad_tokens, down_other)))
    hidden_grad = low(against(grad_tokens, down_own) + hidden_sent.astype(wide)).astype(wide)

    normed_two, inverse_two = norm_forward(after_mixer, feed_scale)
    tokens_two = row_gather(normed_two)
    feed_sent = swapped(low(product(tokens_two, feed_other)))
    feed_raw = product(tokens_two, feed_own) + feed_sent.astype(wide)
    gate, upper = jnp.split(feed_raw, 2, axis=1)
    sigma = jax.nn.sigmoid(gate)
    hidden = low(gate * sigma * upper)
    feed_grad = jnp.concatenate(
        [
            low(hidden_grad * upper * sigma * (1.0 + gate * (1.0 - sigma))),
            low(hidden_grad * gate * sigma),
        ],
        axis=1,
    )
    feed_grad_other = swapped(feed_grad)
    hidden_other = swapped(hidden)
    back_part = low(against(feed_grad, feed_own) + against(feed_grad_other, feed_other))
    mixed_grad, feed_gain_grad = norm_backward(
        after_mixer, inverse_two, feed_scale, row_scatter(back_part)
    )
    mixer_grad = output_grad.astype(wide) + mixed_grad
    mixer_tokens = row_reorder(row_gather(low(mixer_grad)))
    block_output = after_mixer + row_scatter(
        low(product(hidden, down_own) + product(hidden_other, down_other))
    )
    feed_wgrads = outer(
        tokens_two, jnp.concatenate([feed_grad, feed_grad_other], axis=1)
    )
    feed_own_wgrad, feed_other_wgrad = jnp.split(feed_wgrads, 2, axis=1)
    feed_total = dp_sum(in_order(feed_own_wgrad, feed_other_wgrad, 1))
    down_total = dp_sum(outer(in_order(hidden, hidden_other, 1), grad_tokens))

    feature_sent = swapped(low(against(mixer_tokens, out_other)))
    feature_grad = low(against(mixer_tokens, out_own) + feature_sent.astype(wide))
    out_total = dp_sum(outer(in_order(features, features_other, 1), mixer_tokens))
    query_back, pair_back = attend_backward(document_ids, attend_saved, feature_grad[:, channels:])
    (
        input_back, gate_back, step_back, state_back, filter_wgrad, shift_wgrad,
        state_filter_grad, state_shift_grad, bias_wgrad, decay_wgrad, skip_wgrad,
    ) = mamba_backward(mamba_saved, feature_grad[:, :channels], taps)

    proj_back = jnp.pad(
        jnp.concatenate([gate_back, input_back, query_back, low(step_back)], axis=1),
        ((0, 0), (0, spare)),
    )
    proj_back_other = swapped(proj_back)
    common_back = jnp.concatenate([state_back, pair_back], axis=1)
    common_back = low(common_back.astype(wide) + swapped(common_back).astype(wide))
    input_part = low(
        against(common_back, common)
        + against(proj_back, proj_own)
        + against(proj_back_other, proj_other)
    )
    input_norm_grad, mixer_gain_grad = norm_backward(
        residual, inverse_one, mixer_scale, row_scatter(row_reorder(input_part))
    )
    input_grad = mixer_grad + input_norm_grad

    common_wgrad = low(outer(tokens_one, common_back))
    empty = jnp.zeros(key_weight.shape, jnp.bfloat16)
    spread = jnp.concatenate(
        [
            common_wgrad[:, :double],
            lax.dynamic_update_slice_in_dim(
                empty, common_wgrad[:, double : double + HD], pair_head * HD, 1
            ),
            lax.dynamic_update_slice_in_dim(
                empty, common_wgrad[:, double + HD :], pair_head * HD, 1
            ),
        ],
        axis=1,
    )
    model, total_width = spread.shape
    quarter = total_width // 4
    stacked = spread.reshape(model, 4, quarter).swapaxes(0, 1).reshape(4 * model, quarter)
    shared_part = row_scatter(row_reorder(stacked))
    mine_wgrad = outer(tokens_one, proj_back)
    other_wgrad = outer(tokens_one, proj_back_other)
    proj_total = dp_sum(
        jnp.concatenate([in_order(mine_wgrad, other_wgrad, 1), shared_part], axis=1)
    )
    block = sum(spans) + spare
    proj_grads = [
        jnp.concatenate(
            [proj_total[:, edges[k] : edges[k + 1]],
             proj_total[:, block + edges[k] : block + edges[k + 1]]], axis=1,
        )
        for k in range(4)
    ]
    shared = row_reorder(row_gather(low(proj_total[:, 2 * block :])))
    shared = shared.reshape(4, model, quarter).swapaxes(0, 1).reshape(model, total_width)
    shared = shared.astype(wide)
    key_end = double + key_weight.shape[1]

    state_parts = packed([state_filter_grad, state_shift_grad])
    state_parts = state_parts + swapped(state_parts)
    split_at = state_parts.shape[0]
    both_parts = vector_sum(
        jnp.concatenate([state_parts, packed([feed_gain_grad])], axis=0), "row"
    )
    local = [filter_wgrad, shift_wgrad, bias_wgrad, decay_wgrad, skip_wgrad]
    all_parts = vector_sum(jnp.concatenate([both_parts, packed(local)], axis=0), "dp")
    filter_total, state_shift_total = unpacked(
        all_parts[:split_at], [state_filter_grad.shape, state_shift_grad.shape]
    )
    feed_gain_total = unpacked(all_parts[split_at : both_parts.shape[0]], [feed_gain_grad.shape])[0]
    local_totals = unpacked(all_parts[both_parts.shape[0] :], [part.shape for part in local])
    gain_total = vector_sum(vector_sum(packed([mixer_gain_grad]), "row"), "dp")
    gain_total = unpacked(gain_total, [mixer_gain_grad.shape])[0]
    feed_half = feed_gate.shape[1] // 2
    return (
        block_output,
        input_grad,
        gain_total,
        proj_grads[0],
        proj_grads[1],
        proj_grads[3],
        proj_grads[2],
        shared[:, double:key_end],
        shared[:, key_end:],
        shared[:, :double],
        local_totals[0],
        local_totals[1],
        filter_total,
        state_shift_total,
        local_totals[2],
        local_totals[3],
        local_totals[4],
        out_total,
        feed_gain_total,
        jnp.concatenate(
            [feed_total[:, :feed_half], feed_total[:, 2 * feed_half : 3 * feed_half]], axis=1
        ),
        jnp.concatenate(
            [feed_total[:, feed_half : 2 * feed_half], feed_total[:, 3 * feed_half :]], axis=1
        ),
        down_total,
    )


def solution(mesh):
    placed = (
        P(("dp", "row"), "col"),
        P(("dp", "row"), "col"),
        P("dp", None),
        P("col"),
        P("col", "row"),
        P("col", "row"),
        P("col", "row"),
        P("col", "row"),
        P("col", None),
        P("col", None),
        P("col", None),
        P(("row", "col"), None),
        P(("row", "col")),
        P(),
        P(),
        P(("row", "col")),
        P(("row", "col")),
        P(("row", "col")),
        P("row", "col"),
        P("col"),
        P("col", "row"),
        P("col", "row"),
        P("row", "col"),
    )
    return jax.shard_map(
        on_device,
        mesh=mesh,
        in_specs=placed,
        out_specs=(
            P(("dp", "row"), "col"),
            P(("dp", "row"), "col"),
            P("col"),
            P("col", "row"),
            P("col", "row"),
            P("col", "row"),
            P("col", "row"),
            P("col", None),
            P("col", None),
            P("col", None),
            P(("row", "col"), None),
            P(("row", "col")),
            P(),
            P(),
            P(("row", "col")),
            P(("row", "col")),
            P(("row", "col")),
            P("row", "col"),
            P("col"),
            P("col", "row"),
            P("col", "row"),
            P("row", "col"),
        ),
        check_vma=False,
    )
```
